128 devices in a mesh: blk: 64 (over z, x, y), mc: 2 (over core).
Axes of the slice: x: 4, y: 4, z: 4, core: 2. Of those that a mesh axis runs over, the one named last changes fastest.
Arguments:
- batch_ids: int32 [2048], P('blk'), may hold values from 0 to 16383, as said below
- cond_ids: int32 [2048, 3], P('blk'), may hold values from 0 to 16383, as said below
- home: int32 [16384], replicated, may hold values from 0 to 16383, as said below
- latent: bfloat16 [16384, 32, 256], P('blk', 'mc'), may hold values from -6 to 6
- diag_factor: bfloat16 [2048, 256, 256], P('blk'), may hold values from -0.375 to 0.375
- cond_factor: bfloat16 [2048, 3, 256, 256], P('blk'), may hold values from -0.375 to 0.375
- obs: float32 [2048, 256], P('blk'), may hold values from -6 to 6
- noise_prec: float32 [], replicated, may hold values from 0.5 to 2
Outputs:
- mean_grad: float32 [16384, 256], P('blk', 'mc')
The draws below stay inside these ranges and needn't reach their ends.
Inputs may be any that keep to these rules, and one draw needn't show every extreme that they name: home is a permutation; block b is stored at position home[b], on index home[b] // 256 of blk. `batch_ids`: of the 128 blocks named by one index's rows (each row's own block and its conditioning blocks, repeats counted), at most 5 are stored on any one index of blk. `cond_ids`: counted together with batch_ids as stated there.
All inputs are finite; a program needn't handle non-finite values.
Results may differ from the reference program's by a relative error of at most 0.0029.
Values may be sent and summed in bfloat16 or wider, within the bound.
No kernel may reach another device: no remote copies, remote signals or barrier semaphores. Data moves between devices by JAX's collectives and lax.ppermute only.
A program may use at most 64 MiB of HBM per device.

```python
import math
import jax
import jax.numpy as jnp
from jax import lax

BLOCK = 256
COND = 3
ROWS_DEV = 32
OWNED = 256
DRAWS = 32
ROWS = 2048
BLOCKS = 16384
CAPACITY = 5


def request_plan(base_key):
    owners = BLOCKS // OWNED
    want_count = 4 * ROWS_DEV
    pool_size = owners * CAPACITY
    home_perm = jax.random.permutation(jax.random.fold_in(base_key, 11), BLOCKS).astype(jnp.int32)
    inverse_home = jnp.argsort(home_perm).astype(jnp.int32)
    hot_owner = jax.random.randint(jax.random.fold_in(base_key, 12), (), 0, owners)
    pool_owner = jnp.arange(pool_size, dtype=jnp.int32) // CAPACITY
    order_key = jnp.arange(pool_size, dtype=jnp.int32)
    scores = jax.random.randint(jax.random.fold_in(base_key, 13), (owners, pool_size), 0, 1 << 20) * pool_size + order_key[None, :]
    scores = jnp.where(pool_owner[None, :] == hot_owner, order_key[None, :] - pool_size, scores)
    chosen = jnp.argsort(scores, axis=1)[:, :want_count]
    dest_dev = pool_owner[chosen]
    mix_scores = jax.random.randint(jax.random.fold_in(base_key, 14), (owners, want_count), 0, 1 << 20) * want_count + jnp.arange(want_count, dtype=jnp.int32)[None, :]
    mixing = jnp.argsort(mix_scores, axis=1)
    dest_dev = jnp.take_along_axis(dest_dev, mixing, axis=1)
    slot_idx = jax.random.randint(jax.random.fold_in(base_key, 15), (owners, want_count), 0, OWNED)
    position = (dest_dev * OWNED + slot_idx).reshape(-1)
    block_ids = inverse_home[position].reshape(owners * ROWS_DEV, 4).astype(jnp.int32)
    return (home_perm, block_ids)


def draw_batch_ids(key, part):
    home_perm, block_ids = request_plan(key)
    return block_ids[:, 0]


def draw_cond_ids(key, part):
    home_perm, block_ids = request_plan(key)
    return block_ids[:, 1:]


def draw_home(key, part):
    home_perm, block_ids = request_plan(key)
    return home_perm


def level_of(own_key, extent, pieces, least, high):
    def one(dim, parts):
        steps = jax.random.uniform(jax.random.fold_in(jax.random.fold_in(own_key, 6), dim), (parts,), jnp.float32, least / len(pieces), high / len(pieces))
        return jnp.repeat(jnp.exp(steps), extent[dim] // parts).reshape((-1,) + (1,) * (len(extent) - dim - 1))

    gain = one(*pieces[0])
    for cut in pieces[1:]:
        gain = gain * one(*cut)
    return gain


def scatter_about(rng, dims, spread, reach, split=(), kind=jnp.bfloat16):
    array = spread * jax.random.normal(rng, dims, jnp.float32)
    if split:
        array = array * level_of(rng, dims, split, -0.22, 0.18)
    return jnp.clip(array, -reach, reach).astype(kind)


def setup_inputs(seed: int = 0) -> dict:
    arg_keys = jax.random.split(jax.random.key(seed), 9)
    return {
        "batch_ids": draw_batch_ids(jax.random.fold_in(arg_keys[8], 71), 0),
        "cond_ids": draw_cond_ids(jax.random.fold_in(arg_keys[8], 71), 0),
        "home": draw_home(jax.random.fold_in(arg_keys[8], 71), 0),
        "latent": scatter_about(arg_keys[3], (BLOCKS, DRAWS, BLOCK), 1.0, 6.0, ((0, 64), (1, 2))),
        "diag_factor": scatter_about(arg_keys[4], (ROWS, BLOCK, BLOCK), BLOCK ** -0.5, 0.375, ((0, 64),)),
        "cond_factor": scatter_about(arg_keys[5], (ROWS, COND, BLOCK, BLOCK), BLOCK ** -0.5, 0.375, ((0, 64),)),
        "obs": scatter_about(arg_keys[6], (ROWS, BLOCK), 1.0, 6.0, ((0, 64),), jnp.float32),
        "noise_prec": jnp.clip(jnp.exp(jax.random.uniform(arg_keys[7], (), jnp.float32, math.log(0.5), math.log(2.0))), 0.5, 2.0),
    }


freedom = 4.0


def reference(batch_ids, cond_ids, home, latent, diag_factor, cond_factor, obs, noise_prec):
    own_where = home[batch_ids].astype(jnp.int32)
    cond_where = home[cond_ids].astype(jnp.int32)
    lower_mask = jnp.arange(BLOCK)[:, None] >= jnp.arange(BLOCK)[None, :]
    inverse_draws = 1.0 / DRAWS

    def one_row(packed):
        own_pos, near_pos, diag_block, cond_blocks, seen = packed
        own_panel = latent[own_pos]
        lower_diag = jnp.where(lower_mask, diag_block, jnp.zeros_like(diag_block))
        whitened = jnp.dot(own_panel, lower_diag.T, preferred_element_type=jnp.float32)
        for which in range(COND):
            near_panel = latent[near_pos[which]]
            whitened = whitened + jnp.dot(near_panel, cond_blocks[which].T, preferred_element_type=jnp.float32)
        scored = (freedom + 1.0) * whitened / (freedom + whitened * whitened)
        white_low = scored.astype(jnp.bfloat16)
        back_diag = jnp.dot(white_low, lower_diag, preferred_element_type=jnp.float32)
        likely = noise_prec * (seen[None, :] - own_panel.astype(jnp.float32))
        self_term = jnp.sum(likely - back_diag, axis=0) * inverse_draws
        cond_list = []
        for which in range(COND):
            back_cond = jnp.dot(white_low, cond_blocks[which], preferred_element_type=jnp.float32)
            cond_list.append(-jnp.sum(back_cond, axis=0) * inverse_draws)
        return self_term, jnp.stack(cond_list)

    self_terms, cond_terms = lax.map(one_row, (own_where, cond_where, diag_factor, cond_factor, obs))
    mean_grad = jnp.zeros((BLOCKS, BLOCK), jnp.float32)
    mean_grad = mean_grad.at[own_where].add(self_terms)
    mean_grad = mean_grad.at[cond_where.reshape(-1)].add(cond_terms.reshape(-1, BLOCK))
    return mean_grad
```

```python
import functools

import jax
import jax.numpy as jnp
from jax import lax
from jax.experimental import pallas as pl
from jax.experimental.pallas import tpu as pltpu
from jax.sharding import PartitionSpec as P

freedom = 4.0
vmem = pl.BlockSpec(memory_space=pltpu.VMEM)
smem = pl.BlockSpec(memory_space=pltpu.SMEM)
budget = pltpu.CompilerParams(vmem_limit_bytes=48 * 1024 * 1024)
iota = lax.broadcasted_iota


def plan_kernel(owners, capacity, per_owner, own_ref, near_ref, home_ref, outbox_ref, spot_ref):
    home = home_ref[...]
    high_count, low_count = home.shape
    dest_table = (home // per_owner).astype(jnp.float32).T.astype(jnp.bfloat16)
    slot_table = (home % per_owner).astype(jnp.float32).T.astype(jnp.bfloat16)
    rows = own_ref.shape[1]
    earlier = (iota(jnp.int32, (rows, rows), 0) < iota(jnp.int32, (rows, rows), 1)).astype(jnp.bfloat16)
    high_iota = iota(jnp.int32, (high_count, rows), 0)
    low_iota = iota(jnp.int32, (low_count, rows), 0)
    dest_iota = iota(jnp.int32, (owners, rows), 0)
    before = jnp.zeros((owners, 1), jnp.float32)
    marks = [jnp.zeros((owners, 1), jnp.float32) for _ in range(capacity)]
    for which in range(1 + near_ref.shape[0]):
        ids = own_ref[...] if which == 0 else near_ref[which - 1 : which, :]
        high_hot = (high_iota == ids // low_count).astype(jnp.bfloat16)
        low_hot = low_iota == ids % low_count
        dest = jnp.dot(dest_table, high_hot, preferred_element_type=jnp.float32)
        dest = jnp.sum(jnp.where(low_hot, dest, 0.0), axis=0, keepdims=True)
        slot = jnp.dot(slot_table, high_hot, preferred_element_type=jnp.float32)
        slot = jnp.sum(jnp.where(low_hot, slot, 0.0), axis=0, keepdims=True)
        asked = dest_iota == dest.astype(jnp.int32)
        ranks = before + jnp.dot(asked.astype(jnp.bfloat16), earlier, preferred_element_type=jnp.float32)
        before = before + jnp.sum(asked.astype(jnp.float32), axis=1, keepdims=True)
        for k in range(capacity):
            taken = asked & (ranks == float(k))
            marks[k] = marks[k] + jnp.sum(jnp.where(taken, slot + 1.0, 0.0), axis=1, keepdims=True)
        rank = jnp.sum(jnp.where(asked, ranks, 0.0), axis=0, keepdims=True)
        spot_ref[which : which + 1, :] = (dest * 8.0 + rank).astype(jnp.int32)
    lanes = iota(jnp.int32, (owners, outbox_ref.shape[2]), 1)
    outbox = jnp.full(lanes.shape, -1.0, jnp.float32)
    for k in range(capacity):
        outbox = jnp.where(lanes == k, marks[k] - 1.0, outbox)
    outbox_ref[:, 0, :] = outbox.astype(jnp.int32)


def pack_kernel(slots_ref, latent_ref, out_ref):
    owners, capacity = out_ref.shape[:2]

    def step(dev, carry):
        for k in range(capacity):
            out_ref[dev, k] = latent_ref[jnp.maximum(slots_ref[dev, 0, k], 0)]
        return carry

    lax.fori_loop(0, owners, step, 0, unroll=4)


def score_kernel(spot_ref, fetched_ref, diag_ref, cond_ref, sums_ref):
    row_count, width = diag_ref.shape[:2]
    lower = iota(jnp.int32, (width, width), 0) >= iota(jnp.int32, (width, width), 1)
    turned = (((1,), (1,)), ((), ()))

    def step(row, carry):
        spots = [spot_ref[which, row] for which in range(1 + cond_ref.shape[1])]
        panels = [fetched_ref[spot // 8, spot % 8] for spot in spots]
        factor = jnp.where(lower, diag_ref[row], jnp.zeros((), diag_ref.dtype))
        whitened = lax.dot_general(panels[0], factor, turned, preferred_element_type=jnp.float32)
        for which in range(cond_ref.shape[1]):
            whitened = whitened + lax.dot_general(
                panels[which + 1], cond_ref[row, which], turned, preferred_element_type=jnp.float32
            )
        scored = (freedom + 1.0) * whitened / (freedom + whitened * whitened)
        scored = scored.astype(jnp.bfloat16).astype(jnp.float32)
        sums_ref[0, pl.ds(row, 1), :] = jnp.sum(scored, axis=0, keepdims=True)
        sums_ref[1, pl.ds(row, 1), :] = jnp.sum(panels[0].astype(jnp.float32), axis=0, keepdims=True)
        return carry

    lax.fori_loop(0, row_count, step, 0, unroll=2)


def term_kernel(draws, spot_ref, noise_ref, mine_ref, other_ref, obs_ref, diag_ref, cond_ref, out_ref, likely_ref):
    row_count, width = diag_ref.shape[:2]
    half = out_ref.shape[2]
    first = pl.multiple_of(lax.axis_index("mc") * half, half)
    lower = iota(jnp.int32, (width, half), 0) >= iota(jnp.int32, (width, half), 1) + first
    inverse_draws = 1.0 / draws
    which_row = iota(jnp.int32, (16, width), 0)
    out_ref[...] = jnp.zeros_like(out_ref)
    part = pl.ds(first, half)
    owned = mine_ref[1, :, part] + other_ref[1, :, part]
    likely_ref[...] = noise_ref[0, 0] * (obs_ref[:, part] * float(draws) - owned)

    def step(row, carry):
        total = mine_ref[0, pl.ds(row, 1), :] + other_ref[0, pl.ds(row, 1), :]
        coarse = total.astype(jnp.bfloat16).astype(jnp.float32)
        pieces = jnp.where(which_row == 0, coarse, jnp.where(which_row == 1, total - coarse, 0.0))
        pieces = pieces.astype(jnp.bfloat16)
        likely = likely_ref[pl.ds(row, 1), :]
        for which in range(1 + cond_ref.shape[1]):
            if which == 0:
                factor = diag_ref[row, :, part]
                factor = jnp.where(lower, factor, jnp.zeros((), factor.dtype))
            else:
                factor = cond_ref[row, which - 1, :, part]
            back = jnp.dot(pieces, factor, preferred_element_type=jnp.float32)
            back = jnp.sum(back, axis=0, keepdims=True)
            term = (likely - back) * inverse_draws if which == 0 else -back * inverse_draws
            spot = spot_ref[which, row]
            out_ref[spot // 8, pl.ds(spot % 8, 1), :] = term
        return carry

    lax.fori_loop(0, row_count, step, 0, unroll=2)


def gather_kernel(slots_ref, inbox_ref, out_ref):
    owners, capacity, half = inbox_ref.shape
    per_owner = out_ref.shape[0]
    slots = slots_ref[:, 0, :].astype(jnp.float32).T
    places = iota(jnp.int32, (per_owner, owners), 0).astype(jnp.float32)
    total = jnp.zeros((per_owner, half), jnp.float32)
    for k in range(capacity):
        hot = (places == slots[k : k + 1, :]).astype(jnp.bfloat16)
        rest = inbox_ref[:, k, :]
        for _ in range(3):
            piece = rest.astype(jnp.bfloat16)
            rest = rest - piece.astype(jnp.float32)
            total = total + jnp.dot(hot, piece, preferred_element_type=jnp.float32)
    out_ref[...] = total


def body(batch_ids, cond_ids, home, latent, diag_factor, cond_factor, obs, noise_prec):
    owners = lax.axis_size("blk")
    groups = lax.axis_size("mc")
    per_owner, draw_count, width = latent.shape
    row_count = batch_ids.shape[0]
    want_kinds = 1 + cond_ids.shape[1]
    capacity = max(2, 10 * row_count // owners)
    draws = draw_count * groups
    half = width // groups

    def swap(values):
        return lax.all_to_all(values, "blk", split_axis=0, concat_axis=0, tiled=True)

    outbox, spot = pl.pallas_call(
        functools.partial(plan_kernel, owners, capacity, per_owner),
        out_shape=(
            jax.ShapeDtypeStruct((owners, 1, 128), jnp.int32),
            jax.ShapeDtypeStruct((want_kinds, row_count), jnp.int32),
        ),
        in_specs=[vmem] * 3,
        out_specs=(vmem, vmem),
        name="plan",
    )(batch_ids.reshape(1, row_count), cond_ids.T, home.reshape(-1, 128))
    slots = swap(outbox)
    outgoing = pl.pallas_call(
        pack_kernel,
        out_shape=jax.ShapeDtypeStruct((owners, capacity, draw_count, width), latent.dtype),
        in_specs=[smem, vmem],
        out_specs=vmem,
        compiler_params=budget,
        name="pack",
    )(slots, latent)
    fetched = swap(outgoing)
    sums = pl.pallas_call(
        score_kernel,
        out_shape=jax.ShapeDtypeStruct((2, row_count, width), jnp.float32),
        in_specs=[smem, vmem, vmem, vmem],
        out_specs=vmem,
        compiler_params=budget,
        name="score",
    )(spot, fetched, diag_factor, cond_factor)
    others = lax.ppermute(sums, "mc", [(0, 1), (1, 0)])
    terms = pl.pallas_call(
        functools.partial(term_kernel, draws),
        out_shape=jax.ShapeDtypeStruct((owners, capacity, half), jnp.float32),
        in_specs=[smem, smem] + [vmem] * 5,
        out_specs=vmem,
        scratch_shapes=[pltpu.VMEM((row_count, half), jnp.float32)],
        compiler_params=budget,
        name="terms",
    )(spot, noise_prec.reshape(1, 1), sums, others, obs, diag_factor, cond_factor)
    inbox = swap(terms)
    return pl.pallas_call(
        gather_kernel,
        out_shape=jax.ShapeDtypeStruct((per_owner, half), jnp.float32),
        in_specs=[vmem] * 2,
        out_specs=vmem,
        name="collect",
    )(slots, inbox)


def solution(mesh):
    placed = (
        P("blk"),
        P("blk", None),
        P(),
        P("blk", "mc", None),
        P("blk", None, None),
        P("blk", None, None, None),
        P("blk", None),
        P(),
    )
    return jax.shard_map(
        body, mesh=mesh, in_specs=placed, out_specs=P("blk", "mc"), check_vma=False
    )
```

```python
import functools

import jax
import jax.numpy as jnp
from jax import lax
from jax.experimental import pallas as pl
from jax.experimental.pallas import tpu as pltpu
from jax.sharding import PartitionSpec as P

freedom = 4.0
vmem = pl.BlockSpec(memory_space=pltpu.VMEM)
smem = pl.BlockSpec(memory_space=pltpu.SMEM)
anywhere = pl.BlockSpec(memory_space=pl.ANY)
iota = lax.broadcasted_iota


def budget(megabytes):
    return pltpu.CompilerParams(vmem_limit_bytes=megabytes * 1024 * 1024)


def in_hbm(values):
    return pltpu.with_memory_space_constraint(values, pltpu.HBM)


def plan_kernel(
    owners, capacity, own_hbm, near_hbm, home_hbm, latent_hbm, outbox_ref, spot_ref, latent_ref, own_ref, near_ref, home_ref, sems
):
    per_owner = latent_ref.shape[0]
    copies = [
        pltpu.make_async_copy(home_hbm, home_ref, sems.at[0]),
        pltpu.make_async_copy(own_hbm, own_ref, sems.at[1]),
        pltpu.make_async_copy(near_hbm, near_ref, sems.at[2]),
        pltpu.make_async_copy(latent_hbm, latent_ref, sems.at[3]),
    ]
    for copy in copies:
        copy.start()
    for copy in copies[:3]:
        copy.wait()
    home = home_ref[...]
    high_count, low_count = home.shape
    dest_table = (home // per_owner).astype(jnp.float32).T.astype(jnp.bfloat16)
    slot_table = (home % per_owner).astype(jnp.float32).T.astype(jnp.bfloat16)
    rows = own_ref.shape[1]
    earlier = (iota(jnp.int32, (rows, rows), 0) < iota(jnp.int32, (rows, rows), 1)).astype(jnp.bfloat16)
    high_iota = iota(jnp.int32, (high_count, rows), 0)
    low_iota = iota(jnp.int32, (low_count, rows), 0)
    dest_iota = iota(jnp.int32, (owners, rows), 0)
    before = jnp.zeros((owners, 1), jnp.float32)
    marks = [jnp.zeros((owners, 1), jnp.float32) for _ in range(capacity)]
    for which in range(1 + near_ref.shape[0]):
        ids = own_ref[...] if which == 0 else near_ref[which - 1 : which, :]
        high_hot = (high_iota == ids // low_count).astype(jnp.bfloat16)
        low_hot = low_iota == ids % low_count
        dest = jnp.dot(dest_table, high_hot, preferred_element_type=jnp.float32)
        dest = jnp.sum(jnp.where(low_hot, dest, 0.0), axis=0, keepdims=True)
        slot = jnp.dot(slot_table, high_hot, preferred_element_type=jnp.float32)
        slot = jnp.sum(jnp.where(low_hot, slot, 0.0), axis=0, keepdims=True)
        asked = dest_iota == dest.astype(jnp.int32)
        ranks = before + jnp.dot(asked.astype(jnp.bfloat16), earlier, preferred_element_type=jnp.float32)
        before = before + jnp.sum(asked.astype(jnp.float32), axis=1, keepdims=True)
        for k in range(capacity):
            taken = asked & (ranks == float(k))
            marks[k] = marks[k] + jnp.sum(jnp.where(taken, slot + 1.0, 0.0), axis=1, keepdims=True)
        rank = jnp.sum(jnp.where(asked, ranks, 0.0), axis=0, keepdims=True)
        spot_ref[which : which + 1, :] = (dest * 8.0 + rank).astype(jnp.int32)
    lanes = iota(jnp.int32, (owners, outbox_ref.shape[2]), 1)
    outbox = jnp.full(lanes.shape, -1.0, jnp.float32)
    for k in range(capacity):
        outbox = jnp.where(lanes == k, marks[k] - 1.0, outbox)
    outbox_ref[:, 0, :] = outbox.astype(jnp.int32)
    copies[3].wait()


def pack_kernel(slots_ref, latent_ref, out_ref):
    owners, capacity = out_ref.shape[:2]

    def step(dev, carry):
        for k in range(capacity):
            out_ref[dev, k] = latent_ref[jnp.maximum(slots_ref[dev, 0, k], 0)]
        return carry

    lax.fori_loop(0, owners, step, 0, unroll=4)


def score_kernel(chunk, spot_ref, fetched_ref, diag_hbm, cond_hbm, sums_ref, diag_ref, cond_ref, sems):
    row_count, width = diag_ref.shape[:2]
    lower = iota(jnp.int32, (width, width), 0) >= iota(jnp.int32, (width, width), 1)
    turned = (((1,), (1,)), ((), ()))

    def copies(index):
        part = pl.ds(index * chunk, chunk)
        return (
            pltpu.make_async_copy(diag_hbm.at[part], diag_ref.at[part], sems.at[0, index]),
            pltpu.make_async_copy(cond_hbm.at[part], cond_ref.at[part], sems.at[1, index]),
        )

    for index in range(row_count // chunk):
        for copy in copies(index):
            copy.start()

    def score(row):
        spots = [spot_ref[which, row] for which in range(1 + cond_ref.shape[1])]
        panels = [fetched_ref[spot // 8, spot % 8] for spot in spots]
        factor = jnp.where(lower, diag_ref[row], jnp.zeros((), diag_ref.dtype))
        whitened = lax.dot_general(panels[0], factor, turned, preferred_element_type=jnp.float32)
        for which in range(cond_ref.shape[1]):
            whitened = whitened + lax.dot_general(
                panels[which + 1], cond_ref[row, which], turned, preferred_element_type=jnp.float32
            )
        scored = (freedom + 1.0) * whitened / (freedom + whitened * whitened)
        scored = scored.astype(jnp.bfloat16).astype(jnp.float32)
        sums_ref[0, pl.ds(row, 1), :] = jnp.sum(scored, axis=0, keepdims=True)
        sums_ref[1, pl.ds(row, 1), :] = jnp.sum(panels[0].astype(jnp.float32), axis=0, keepdims=True)

    def step(index, carry):
        for copy in copies(index):
            copy.wait()
        for i in range(chunk):
            score(index * chunk + i)
        return carry

    lax.fori_loop(0, row_count // chunk, step, 0)


def term_kernel(
    draws, chunk, spot_ref, noise_ref, mine_ref, other_ref, obs_ref, diag_hbm, cond_hbm, out_ref, likely_ref, diag_ref, cond_ref, sems
):
    row_count, width, half = diag_ref.shape
    first = pl.multiple_of(lax.axis_index("mc") * half, half)
    columns = pl.ds(first, half)

    def copies(index):
        part = pl.ds(index * chunk, chunk)
        return (
            pltpu.make_async_copy(diag_hbm.at[part, :, columns], diag_ref.at[part], sems.at[0, index]),
            pltpu.make_async_copy(cond_hbm.at[part, :, :, columns], cond_ref.at[part], sems.at[1, index]),
        )

    for index in range(row_count // chunk):
        for copy in copies(index):
            copy.start()

    lower = iota(jnp.int32, (width, half), 0) >= iota(jnp.int32, (width, half), 1) + first
    inverse_draws = 1.0 / draws
    which_row = iota(jnp.int32, (16, width), 0)
    out_ref[...] = jnp.zeros_like(out_ref)
    owned = mine_ref[1, :, columns] + other_ref[1, :, columns]
    likely_ref[...] = noise_ref[0, 0] * (obs_ref[:, columns] * float(draws) - owned)

    def term(row):
        total = mine_ref[0, pl.ds(row, 1), :] + other_ref[0, pl.ds(row, 1), :]
        coarse = total.astype(jnp.bfloat16).astype(jnp.float32)
        pieces = jnp.where(which_row == 0, coarse, jnp.where(which_row == 1, total - coarse, 0.0))
        pieces = pieces.astype(jnp.bfloat16)
        for which in range(1 + cond_ref.shape[1]):
            if which == 0:
                factor = jnp.where(lower, diag_ref[row], jnp.zeros((), diag_ref.dtype))
            else:
                factor = cond_ref[row, which - 1]
            back = jnp.dot(pieces, factor, preferred_element_type=jnp.float32)
            back = back[0:1] + back[1:2]
            if which == 0:
                back = back - likely_ref[pl.ds(row, 1), :]
            spot = spot_ref[which, row]
            out_ref[spot // 8, pl.ds(spot % 8, 1), :] = back * -inverse_draws

    def step(index, carry):
        for copy in copies(index):
            copy.wait()
        for i in range(chunk):
            term(index * chunk + i)
        return carry

    lax.fori_loop(0, row_count // chunk, step, 0)


def gather_kernel(slots_ref, inbox_ref, out_ref):
    owners, capacity, half = inbox_ref.shape
    per_owner = out_ref.shape[0]
    slots = slots_ref[:, 0, :].astype(jnp.float32).T
    places = iota(jnp.int32, (per_owner, owners), 0).astype(jnp.float32)
    total = jnp.zeros((per_owner, half), jnp.float32)
    for k in range(capacity):
        hot = (places == slots[k : k + 1, :]).astype(jnp.bfloat16)
        rest = inbox_ref[:, k, :]
        for _ in range(3):
            piece = rest.astype(jnp.bfloat16)
            rest = rest - piece.astype(jnp.float32)
            total = total + jnp.dot(hot, piece, preferred_element_type=jnp.float32)
    out_ref[...] = total


def body(batch_ids, cond_ids, home, latent, diag_factor, cond_factor, obs, noise_prec):
    owners = lax.axis_size("blk")
    groups = lax.axis_size("mc")
    per_owner, draw_count, width = latent.shape
    row_count = batch_ids.shape[0]
    want_kinds = 1 + cond_ids.shape[1]
    capacity = max(2, 10 * row_count // owners)
    draws = draw_count * groups
    half = width // groups

    def swap(values):
        return lax.all_to_all(values, "blk", split_axis=0, concat_axis=0, tiled=True)

    outbox, spot, staged = pl.pallas_call(
        functools.partial(plan_kernel, owners, capacity),
        out_shape=(
            jax.ShapeDtypeStruct((owners, 1, 128), jnp.int32),
            jax.ShapeDtypeStruct((want_kinds, row_count), jnp.int32),
            pltpu.VMEM(latent.shape, latent.dtype),
        ),
        in_specs=[anywhere] * 4,
        out_specs=(vmem,) * 3,
        scratch_shapes=[
            pltpu.VMEM((1, row_count), jnp.int32),
            pltpu.VMEM((want_kinds - 1, row_count), jnp.int32),
            pltpu.VMEM((home.shape[0] // 128, 128), jnp.int32),
            pltpu.SemaphoreType.DMA((4,)),
        ],
        compiler_params=budget(16),
        name="plan",
    )(in_hbm(batch_ids.reshape(1, row_count)), in_hbm(cond_ids.T), in_hbm(home.reshape(-1, 128)), in_hbm(latent))
    slots = swap(outbox)
    outgoing = pl.pallas_call(
        pack_kernel,
        out_shape=jax.ShapeDtypeStruct((owners, capacity, draw_count, width), latent.dtype),
        in_specs=[smem, vmem],
        out_specs=vmem,
        compiler_params=budget(16),
        name="pack",
    )(slots, staged)
    fetched = swap(outgoing)
    diag_factor, cond_factor, obs = in_hbm(diag_factor), in_hbm(cond_factor), in_hbm(obs)
    sums = pl.pallas_call(
        functools.partial(score_kernel, 8),
        out_shape=jax.ShapeDtypeStruct((2, row_count, width), jnp.float32),
        in_specs=[smem, vmem, anywhere, anywhere],
        out_specs=vmem,
        scratch_shapes=[
            pltpu.VMEM(diag_factor.shape, diag_factor.dtype),
            pltpu.VMEM(cond_factor.shape, cond_factor.dtype),
            pltpu.SemaphoreType.DMA((2, row_count // 8)),
        ],
        compiler_params=budget(32),
        name="score",
    )(spot, fetched, diag_factor, cond_factor)
    others = lax.ppermute(sums, "mc", [(0, 1), (1, 0)])
    terms = pl.pallas_call(
        functools.partial(term_kernel, draws, 4),
        out_shape=jax.ShapeDtypeStruct((owners, capacity, half), jnp.float32),
        in_specs=[smem, smem, vmem, vmem, vmem, anywhere, anywhere],
        out_specs=vmem,
        scratch_shapes=[
            pltpu.VMEM((row_count, half), jnp.float32),
            pltpu.VMEM((row_count, width, half), diag_factor.dtype),
            pltpu.VMEM((row_count, want_kinds - 1, width, half), cond_factor.dtype),
            pltpu.SemaphoreType.DMA((2, row_count // 4)),
        ],
        compiler_params=budget(32),
        name="terms",
    )(spot, noise_prec.reshape(1, 1), sums, others, obs, diag_factor, cond_factor)
    inbox = swap(terms)
    return pl.pallas_call(
        gather_kernel,
        out_shape=jax.ShapeDtypeStruct((per_owner, half), jnp.float32),
        in_specs=[vmem] * 2,
        out_specs=vmem,
        compiler_params=budget(16),
        name="collect",
    )(slots, inbox)


def solution(mesh):
    placed = (
        P("blk"),
        P("blk", None),
        P(),
        P("blk", "mc", None),
        P("blk", None, None),
        P("blk", None, None, None),
        P("blk", None),
        P(),
    )
    return jax.shard_map(
        body, mesh=mesh, in_specs=placed, out_specs=P("blk", "mc"), check_vma=False
    )
```

```python
import functools

import jax
import jax.numpy as jnp
from jax import lax
from jax.experimental import pallas as pl
from jax.experimental.pallas import tpu as pltpu
from jax.sharding import PartitionSpec as P

freedom = 4.0
vmem = pl.BlockSpec(memory_space=pltpu.VMEM)
smem = pl.BlockSpec(memory_space=pltpu.SMEM)
anywhere = pl.BlockSpec(memory_space=pl.ANY)
iota = lax.broadcasted_iota


def budget(megabytes):
    return pltpu.CompilerParams(vmem_limit_bytes=megabytes * 1024 * 1024)


def in_hbm(values):
    return pltpu.with_memory_space_constraint(values, pltpu.HBM)


def in_vmem(values):
    return pltpu.with_memory_space_constraint(values, pltpu.VMEM)


def plan_kernel(
    owners, capacity, noise_ref, own_hbm, near_hbm, home_hbm, latent_hbm, outbox_ref, spot_ref, noise_row_ref, latent_ref, own_ref, near_ref, home_ref, sems
):
    per_owner = latent_ref.shape[0]
    copies = [
        pltpu.make_async_copy(home_hbm, home_ref, sems.at[0]),
        pltpu.make_async_copy(own_hbm, own_ref, sems.at[1]),
        pltpu.make_async_copy(near_hbm, near_ref, sems.at[2]),
        pltpu.make_async_copy(latent_hbm, latent_ref, sems.at[3]),
    ]
    for copy in copies:
        copy.start()
    for copy in copies[:3]:
        copy.wait()
    home = home_ref[...]
    high_count, low_count = home.shape
    dest_table = (home // per_owner).astype(jnp.float32).T.astype(jnp.bfloat16)
    slot_table = (home % per_owner).astype(jnp.float32).T.astype(jnp.bfloat16)
    rows = own_ref.shape[1]
    earlier = (iota(jnp.int32, (rows, rows), 0) < iota(jnp.int32, (rows, rows), 1)).astype(jnp.bfloat16)
    high_iota = iota(jnp.int32, (high_count, rows), 0)
    low_iota = iota(jnp.int32, (low_count, rows), 0)
    dest_iota = iota(jnp.int32, (owners, rows), 0)
    before = jnp.zeros((owners, 1), jnp.float32)
    marks = [jnp.zeros((owners, 1), jnp.float32) for _ in range(capacity)]
    for which in range(1 + near_ref.shape[0]):
        ids = own_ref[...] if which == 0 else near_ref[which - 1 : which, :]
        high_hot = (high_iota == ids // low_count).astype(jnp.bfloat16)
        low_hot = low_iota == ids % low_count
        dest = jnp.dot(dest_table, high_hot, preferred_element_type=jnp.float32)
        dest = jnp.sum(jnp.where(low_hot, dest, 0.0), axis=0, keepdims=True)
        slot = jnp.dot(slot_table, high_hot, preferred_element_type=jnp.float32)
        slot = jnp.sum(jnp.where(low_hot, slot, 0.0), axis=0, keepdims=True)
        asked = dest_iota == dest.astype(jnp.int32)
        ranks = before + jnp.dot(asked.astype(jnp.bfloat16), earlier, preferred_element_type=jnp.float32)
        before = before + jnp.sum(asked.astype(jnp.float32), axis=1, keepdims=True)
        for k in range(capacity):
            taken = asked & (ranks == float(k))
            marks[k] = marks[k] + jnp.sum(jnp.where(taken, slot + 1.0, 0.0), axis=1, keepdims=True)
        rank = jnp.sum(jnp.where(asked, ranks, 0.0), axis=0, keepdims=True)
        spot_ref[which : which + 1, :] = (dest * 8.0 + rank).astype(jnp.int32)
    lanes = iota(jnp.int32, (owners, outbox_ref.shape[2]), 1)
    outbox = jnp.full(lanes.shape, -1.0, jnp.float32)
    for k in range(capacity):
        outbox = jnp.where(lanes == k, marks[k] - 1.0, outbox)
    outbox_ref[:, 0, :] = outbox.astype(jnp.int32)
    noise_row_ref[...] = jnp.full(noise_row_ref.shape, noise_ref[0], jnp.float32)
    copies[3].wait()


def pack_kernel(slots_ref, latent_ref, out_ref):
    owners, capacity = out_ref.shape[:2]

    def step(dev, carry):
        for k in range(capacity):
            out_ref[dev, k] = latent_ref[jnp.maximum(slots_ref[dev, 0, k], 0)]
        return carry

    lax.fori_loop(0, owners, step, 0, unroll=4)


def score_kernel(
    chunk, spot_ref, noise_ref, obs_ref, fetched_ref, diag_ref, cond_ref, sums_ref, diag_half_ref, cond_half_ref
):
    noise = noise_ref[...]
    draw_count = float(fetched_ref.shape[2])
    row_count, width = diag_ref.shape[:2]
    lower = iota(jnp.int32, (width, width), 0) >= iota(jnp.int32, (width, width), 1)
    turned = (((1,), (1,)), ((), ()))
    half = diag_half_ref.shape[2]
    columns = pl.ds(pl.multiple_of(lax.axis_index("mc") * half, half), half)

    def score(row):
        spots = [spot_ref[which, row] for which in range(1 + cond_ref.shape[1])]
        panels = [fetched_ref[spot // 8, spot % 8] for spot in spots]
        factor = jnp.where(lower, diag_ref[row], jnp.zeros((), diag_ref.dtype))
        diag_half_ref[row] = diag_ref[row, :, columns]
        for which in range(cond_ref.shape[1]):
            cond_half_ref[row, which] = cond_ref[row, which, :, columns]
        whitened = lax.dot_general(panels[0], factor, turned, preferred_element_type=jnp.float32)
        for which in range(cond_ref.shape[1]):
            whitened = whitened + lax.dot_general(
                panels[which + 1], cond_ref[row, which], turned, preferred_element_type=jnp.float32
            )
        scored = (freedom + 1.0) * whitened / (freedom + whitened * whitened)
        scored = scored.astype(jnp.bfloat16).astype(jnp.float32)
        sums_ref[0, pl.ds(row, 1), :] = jnp.sum(scored, axis=0, keepdims=True)
        owned = jnp.sum(panels[0].astype(jnp.float32), axis=0, keepdims=True)
        sums_ref[1, pl.ds(row, 1), :] = noise * (obs_ref[pl.ds(row, 1), :] * draw_count - owned)

    def step(index, carry):
        for i in range(chunk):
            score(index * chunk + i)
        return carry

    lax.fori_loop(0, row_count // chunk, step, 0)


def term_kernel(draws, chunk, spot_ref, mine_ref, other_ref, diag_ref, cond_ref, out_ref, likely_ref):
    row_count, width = diag_ref.shape[:2]
    half = out_ref.shape[2]
    first = pl.multiple_of(lax.axis_index("mc") * half, half)
    columns = pl.ds(first, half)
    lower = iota(jnp.int32, (width, half), 0) >= iota(jnp.int32, (width, half), 1) + first
    inverse_draws = 1.0 / draws
    which_row = iota(jnp.int32, (16, width), 0)
    out_ref[...] = jnp.zeros_like(out_ref)
    likely_ref[...] = mine_ref[1, :, columns] + other_ref[1, :, columns]

    def term(row):
        total = mine_ref[0, pl.ds(row, 1), :] + other_ref[0, pl.ds(row, 1), :]
        coarse = total.astype(jnp.bfloat16).astype(jnp.float32)
        pieces = jnp.where(which_row == 0, coarse, jnp.where(which_row == 1, total - coarse, 0.0))
        pieces = pieces.astype(jnp.bfloat16)
        for which in range(1 + cond_ref.shape[1]):
            if which == 0:
                factor = jnp.where(lower, diag_ref[row], jnp.zeros((), diag_ref.dtype))
            else:
                factor = cond_ref[row, which - 1]
            back = jnp.dot(pieces, factor, preferred_element_type=jnp.float32)
            back = back[0:1] + back[1:2]
            if which == 0:
                back = back - likely_ref[pl.ds(row, 1), :]
            spot = spot_ref[which, row]
            out_ref[spot // 8, pl.ds(spot % 8, 1), :] = back * -inverse_draws

    def step(index, carry):
        for i in range(chunk):
            term(index * chunk + i)
        return carry

    lax.fori_loop(0, row_count // chunk, step, 0)


def gather_kernel(slots_ref, inbox_ref, out_ref):
    owners, capacity, half = inbox_ref.shape
    per_owner = out_ref.shape[0]
    slots = slots_ref[:, 0, :].astype(jnp.float32).T
    places = iota(jnp.int32, (per_owner, owners), 0).astype(jnp.float32)
    total = jnp.zeros((per_owner, half), jnp.float32)
    for k in range(capacity):
        hot = (places == slots[k : k + 1, :]).astype(jnp.bfloat16)
        rest = inbox_ref[:, k, :]
        for _ in range(3):
            piece = rest.astype(jnp.bfloat16)
            rest = rest - piece.astype(jnp.float32)
            total = total + jnp.dot(hot, piece, preferred_element_type=jnp.float32)
    out_ref[...] = total


def body(batch_ids, cond_ids, home, latent, diag_factor, cond_factor, obs, noise_prec):
    owners = lax.axis_size("blk")
    groups = lax.axis_size("mc")
    per_owner, draw_count, width = latent.shape
    row_count = batch_ids.shape[0]
    want_kinds = 1 + cond_ids.shape[1]
    capacity = max(2, 10 * row_count // owners)
    draws = draw_count * groups
    half = width // groups

    def swap(values):
        return lax.all_to_all(values, "blk", split_axis=0, concat_axis=0, tiled=True)

    outbox, spot, noise_row, staged = pl.pallas_call(
        functools.partial(plan_kernel, owners, capacity),
        out_shape=(
            jax.ShapeDtypeStruct((owners, 1, 128), jnp.int32),
            jax.ShapeDtypeStruct((want_kinds, row_count), jnp.int32),
            jax.ShapeDtypeStruct((1, width), jnp.float32),
            pltpu.VMEM(latent.shape, latent.dtype),
        ),
        in_specs=[smem] + [anywhere] * 4,
        out_specs=(vmem,) * 4,
        scratch_shapes=[
            pltpu.VMEM((1, row_count), jnp.int32),
            pltpu.VMEM((want_kinds - 1, row_count), jnp.int32),
            pltpu.VMEM((home.shape[0] // 128, 128), jnp.int32),
            pltpu.SemaphoreType.DMA((4,)),
        ],
        compiler_params=budget(16),
        name="plan",
    )(noise_prec.reshape(1), in_hbm(batch_ids.reshape(1, row_count)), in_hbm(cond_ids.T), in_hbm(home.reshape(-1, 128)), in_hbm(latent))
    slots = swap(outbox)
    outgoing = pl.pallas_call(
        pack_kernel,
        out_shape=jax.ShapeDtypeStruct((owners, capacity, draw_count, width), latent.dtype),
        in_specs=[smem, vmem],
        out_specs=vmem,
        compiler_params=budget(8),
        cost_estimate=pl.CostEstimate(flops=10**11, transcendentals=0, bytes_accessed=10**8),
        name="pack",
    )(slots, staged)
    fetched = swap(outgoing)
    diag_here, cond_here, obs = in_vmem(diag_factor), in_vmem(cond_factor), in_hbm(obs)
    sums, diag_half, cond_half = pl.pallas_call(
        functools.partial(score_kernel, 8),
        out_shape=(
            jax.ShapeDtypeStruct((2, row_count, width), jnp.float32),
            jax.ShapeDtypeStruct((row_count, width, half), diag_factor.dtype),
            jax.ShapeDtypeStruct((row_count, want_kinds - 1, width, half), cond_factor.dtype),
        ),
        in_specs=[smem] + [vmem] * 5,
        out_specs=(vmem,) * 3,
        compiler_params=budget(12),
        name="score",
    )(spot, noise_row, obs, fetched, diag_here, cond_here)
    others = lax.ppermute(sums, "mc", [(0, 1), (1, 0)])
    terms = pl.pallas_call(
        functools.partial(term_kernel, draws, 4),
        out_shape=jax.ShapeDtypeStruct((owners, capacity, half), jnp.float32),
        in_specs=[smem] + [vmem] * 4,
        out_specs=vmem,
        scratch_shapes=[pltpu.VMEM((row_count, half), jnp.float32)],
        compiler_params=budget(12),
        name="terms",
    )(spot, sums, others, diag_half, cond_half)
    inbox = swap(terms)
    return pl.pallas_call(
        gather_kernel,
        out_shape=jax.ShapeDtypeStruct((per_owner, half), jnp.float32),
        in_specs=[vmem] * 2,
        out_specs=vmem,
        compiler_params=budget(16),
        name="collect",
    )(slots, inbox)


def solution(mesh):
    placed = (
        P("blk"),
        P("blk", None),
        P(),
        P("blk", "mc", None),
        P("blk", None, None),
        P("blk", None, None, None),
        P("blk", None),
        P(),
    )
    return jax.shard_map(
        body, mesh=mesh, in_specs=placed, out_specs=P("blk", "mc"), check_vma=False
    )
```

```python
import functools

import jax
import jax.numpy as jnp
from jax import lax
from jax.experimental import pallas as pl
from jax.experimental.pallas import tpu as pltpu
from jax.sharding import PartitionSpec as P

freedom = 4.0
vmem = pl.BlockSpec(memory_space=pltpu.VMEM)
smem = pl.BlockSpec(memory_space=pltpu.SMEM)
anywhere = pl.BlockSpec(memory_space=pl.ANY)
iota = lax.broadcasted_iota


def budget(megabytes):
    return pltpu.CompilerParams(vmem_limit_bytes=megabytes * 1024 * 1024)


def in_hbm(values):
    return pltpu.with_memory_space_constraint(values, pltpu.HBM)


def in_vmem(values):
    return pltpu.with_memory_space_constraint(values, pltpu.VMEM)


def plan_kernel(
    owners, capacity, noise_ref, own_hbm, near_hbm, home_hbm, latent_hbm, outbox_ref, spot_ref, noise_row_ref, latent_ref, own_ref, near_ref, home_ref, sems
):
    per_owner = latent_ref.shape[0]
    copies = [
        pltpu.make_async_copy(home_hbm, home_ref, sems.at[0]),
        pltpu.make_async_copy(own_hbm, own_ref, sems.at[1]),
        pltpu.make_async_copy(near_hbm, near_ref, sems.at[2]),
        pltpu.make_async_copy(latent_hbm, latent_ref, sems.at[3]),
    ]
    for copy in copies:
        copy.start()
    for copy in copies[:3]:
        copy.wait()
    home = home_ref[...]
    high_count, low_count = home.shape
    dest_table = (home // per_owner).astype(jnp.float32).T.astype(jnp.bfloat16)
    slot_table = (home % per_owner).astype(jnp.float32).T.astype(jnp.bfloat16)
    rows = own_ref.shape[1]
    earlier = (iota(jnp.int32, (rows, rows), 0) < iota(jnp.int32, (rows, rows), 1)).astype(jnp.bfloat16)
    high_iota = iota(jnp.int32, (high_count, rows), 0)
    low_iota = iota(jnp.int32, (low_count, rows), 0)
    dest_iota = iota(jnp.int32, (owners, rows), 0)
    before = jnp.zeros((owners, 1), jnp.float32)
    marks = [jnp.zeros((owners, 1), jnp.float32) for _ in range(capacity)]
    for which in range(1 + near_ref.shape[0]):
        ids = own_ref[...] if which == 0 else near_ref[which - 1 : which, :]
        high_hot = (high_iota == ids // low_count).astype(jnp.bfloat16)
        low_hot = low_iota == ids % low_count
        dest = jnp.dot(dest_table, high_hot, preferred_element_type=jnp.float32)
        dest = jnp.sum(jnp.where(low_hot, dest, 0.0), axis=0, keepdims=True)
        slot = jnp.dot(slot_table, high_hot, preferred_element_type=jnp.float32)
        slot = jnp.sum(jnp.where(low_hot, slot, 0.0), axis=0, keepdims=True)
        asked = dest_iota == dest.astype(jnp.int32)
        ranks = before + jnp.dot(asked.astype(jnp.bfloat16), earlier, preferred_element_type=jnp.float32)
        before = before + jnp.sum(asked.astype(jnp.float32), axis=1, keepdims=True)
        for k in range(capacity):
            taken = asked & (ranks == float(k))
            marks[k] = marks[k] + jnp.sum(jnp.where(taken, slot + 1.0, 0.0), axis=1, keepdims=True)
        rank = jnp.sum(jnp.where(asked, ranks, 0.0), axis=0, keepdims=True)
        spot_ref[which : which + 1, :] = (dest * 8.0 + rank).astype(jnp.int32)
    lanes = iota(jnp.int32, (owners, outbox_ref.shape[2]), 1)
    outbox = jnp.full(lanes.shape, -1.0, jnp.float32)
    for k in range(capacity):
        outbox = jnp.where(lanes == k, marks[k] - 1.0, outbox)
    outbox_ref[:, 0, :] = outbox.astype(jnp.int32)
    noise_row_ref[...] = jnp.full(noise_row_ref.shape, noise_ref[0], jnp.float32)
    copies[3].wait()


def pack_kernel(slots_ref, latent_ref, out_ref, turned_ref, scalar_ref, sem):
    owners, capacity = out_ref.shape[:2]
    turned = jnp.maximum(slots_ref[:, 0, :], 0).astype(jnp.float32).T
    turned_ref[:, pl.ds(0, owners)] = turned[: turned_ref.shape[0]].astype(jnp.int32)
    copy = pltpu.make_async_copy(turned_ref, scalar_ref, sem)
    copy.start()
    copy.wait()

    def step(dev, carry):
        for k in range(capacity):
            out_ref[dev, k] = latent_ref[scalar_ref[k, dev]]
        return carry

    lax.fori_loop(0, owners, step, 0, unroll=8)


def score_kernel(
    chunk, spot_ref, noise_ref, obs_ref, fetched_ref, diag_ref, cond_ref, sums_ref
):
    noise = noise_ref[...]
    draw_count = float(fetched_ref.shape[2])
    row_count, width = diag_ref.shape[:2]
    lower = iota(jnp.int32, (width, width), 0) >= iota(jnp.int32, (width, width), 1)
    turned = (((1,), (1,)), ((), ()))

    def score(row):
        spots = [spot_ref[which, row] for which in range(1 + cond_ref.shape[1])]
        panels = [fetched_ref[spot // 8, spot % 8] for spot in spots]
        factor = jnp.where(lower, diag_ref[row], jnp.zeros((), diag_ref.dtype))
        whitened = lax.dot_general(factor, panels[0], turned, preferred_element_type=jnp.float32).T
        for which in range(cond_ref.shape[1]):
            whitened = whitened + lax.dot_general(
                panels[which + 1], cond_ref[row, which], turned, preferred_element_type=jnp.float32
            )
        scored = (freedom + 1.0) * whitened / (freedom + whitened * whitened)
        scored = scored.astype(jnp.bfloat16).astype(jnp.float32)
        sums_ref[0, pl.ds(row, 1), :] = jnp.sum(scored, axis=0, keepdims=True)
        owned = jnp.sum(panels[0].astype(jnp.float32), axis=0, keepdims=True)
        sums_ref[1, pl.ds(row, 1), :] = noise * (obs_ref[pl.ds(row, 1), :] * draw_count - owned)

    def step(index, carry):
        for i in range(chunk):
            score(index * chunk + i)
        return carry

    lax.fori_loop(0, row_count // chunk, step, 0)


def term_kernel(draws, chunk, spot_ref, mine_ref, other_ref, diag_ref, cond_ref, out_ref, likely_ref):
    row_count, width = diag_ref.shape[:2]
    half = out_ref.shape[2]
    first = pl.multiple_of(lax.axis_index("mc") * half, half)
    columns = pl.ds(first, half)
    lower = iota(jnp.int32, (width, half), 0) >= iota(jnp.int32, (width, half), 1) + first
    inverse_draws = 1.0 / draws
    which_row = iota(jnp.int32, (16, width), 0)
    out_ref[...] = jnp.zeros_like(out_ref)
    likely_ref[...] = mine_ref[1, :, columns] + other_ref[1, :, columns]

    def term(row):
        total = mine_ref[0, pl.ds(row, 1), :] + other_ref[0, pl.ds(row, 1), :]
        coarse = total.astype(jnp.bfloat16).astype(jnp.float32)
        pieces = jnp.where(which_row == 0, coarse, jnp.where(which_row == 1, total - coarse, 0.0))
        pieces = pieces.astype(jnp.bfloat16)
        for which in range(1 + cond_ref.shape[1]):
            if which == 0:
                factor = jnp.where(lower, diag_ref[row, :, columns], jnp.zeros((), diag_ref.dtype))
            else:
                factor = cond_ref[row, which - 1, :, columns]
            back = jnp.dot(pieces, factor, preferred_element_type=jnp.float32)
            back = back[0:1] + back[1:2]
            if which == 0:
                back = back - likely_ref[pl.ds(row, 1), :]
            spot = spot_ref[which, row]
            out_ref[spot // 8, pl.ds(spot % 8, 1), :] = back * -inverse_draws

    def step(index, carry):
        for i in range(chunk):
            term(index * chunk + i)
        return carry

    lax.fori_loop(0, row_count // chunk, step, 0)


def gather_kernel(slots_ref, inbox_ref, out_ref):
    owners, capacity, half = inbox_ref.shape
    per_owner = out_ref.shape[0]
    slots = slots_ref[:, 0, :].astype(jnp.float32).T
    slots = jnp.concatenate([slots[k : k + 1, :] for k in range(capacity)], axis=1)
    places = iota(jnp.int32, (per_owner, owners * capacity), 0).astype(jnp.float32)
    hot = (places == slots).astype(jnp.bfloat16)
    rest = jnp.concatenate([inbox_ref[:, k, :] for k in range(capacity)], axis=0)
    total = jnp.zeros((per_owner, half), jnp.float32)
    for _ in range(3):
        piece = rest.astype(jnp.bfloat16)
        rest = rest - piece.astype(jnp.float32)
        total = total + jnp.dot(hot, piece, preferred_element_type=jnp.float32)
    out_ref[...] = total


def body(batch_ids, cond_ids, home, latent, diag_factor, cond_factor, obs, noise_prec):
    owners = lax.axis_size("blk")
    groups = lax.axis_size("mc")
    per_owner, draw_count, width = latent.shape
    row_count = batch_ids.shape[0]
    want_kinds = 1 + cond_ids.shape[1]
    capacity = max(2, 10 * row_count // owners)
    draws = draw_count * groups
    half = width // groups

    def swap(values):
        return lax.all_to_all(values, "blk", split_axis=0, concat_axis=0, tiled=True)

    outbox, spot, noise_row, staged = pl.pallas_call(
        functools.partial(plan_kernel, owners, capacity),
        out_shape=(
            jax.ShapeDtypeStruct((owners, 1, 128), jnp.int32),
            jax.ShapeDtypeStruct((want_kinds, row_count), jnp.int32),
            jax.ShapeDtypeStruct((1, width), jnp.float32),
            pltpu.VMEM(latent.shape, latent.dtype),
        ),
        in_specs=[smem] + [anywhere] * 4,
        out_specs=(vmem,) * 4,
        scratch_shapes=[
            pltpu.VMEM((1, row_count), jnp.int32),
            pltpu.VMEM((want_kinds - 1, row_count), jnp.int32),
            pltpu.VMEM((home.shape[0] // 128, 128), jnp.int32),
            pltpu.SemaphoreType.DMA((4,)),
        ],
        compiler_params=budget(16),
        name="plan",
    )(noise_prec.reshape(1), in_hbm(batch_ids.reshape(1, row_count)), in_hbm(cond_ids.T), in_hbm(home.reshape(-1, 128)), in_hbm(latent))
    slots = swap(outbox)
    outgoing = pl.pallas_call(
        pack_kernel,
        out_shape=jax.ShapeDtypeStruct((owners, capacity, draw_count, width), latent.dtype),
        in_specs=[vmem, vmem],
        out_specs=vmem,
        scratch_shapes=[
            pltpu.VMEM((8, 128), jnp.int32),
            pltpu.SMEM((8, 128), jnp.int32),
            pltpu.SemaphoreType.DMA,
        ],
        compiler_params=budget(8),
        cost_estimate=pl.CostEstimate(flops=10**11, transcendentals=0, bytes_accessed=10**8),
        name="pack",
    )(slots, staged)
    fetched = swap(outgoing)
    diag_here, cond_here, obs = in_vmem(diag_factor), in_vmem(cond_factor), in_hbm(obs)
    sums = pl.pallas_call(
        functools.partial(score_kernel, 16),
        out_shape=jax.ShapeDtypeStruct((2, row_count, width), jnp.float32),
        in_specs=[smem] + [vmem] * 5,
        out_specs=vmem,
        compiler_params=budget(12),
        name="score",
    )(spot, noise_row, obs, fetched, diag_here, cond_here)
    others = lax.ppermute(sums, "mc", [(0, 1), (1, 0)])
    terms = pl.pallas_call(
        functools.partial(term_kernel, draws, 8),
        out_shape=jax.ShapeDtypeStruct((owners, capacity, half), jnp.float32),
        in_specs=[smem] + [vmem] * 4,
        out_specs=vmem,
        scratch_shapes=[pltpu.VMEM((row_count, half), jnp.float32)],
        compiler_params=budget(12),
        name="terms",
    )(spot, sums, others, diag_here, cond_here)
    inbox = swap(terms)
    return pl.pallas_call(
        gather_kernel,
        out_shape=jax.ShapeDtypeStruct((per_owner, half), jnp.float32),
        in_specs=[vmem] * 2,
        out_specs=vmem,
        compiler_params=budget(16),
        name="collect",
    )(slots, inbox)


def solution(mesh):
    placed = (
        P("blk"),
        P("blk", None),
        P(),
        P("blk", "mc", None),
        P("blk", None, None),
        P("blk", None, None, None),
        P("blk", None),
        P(),
    )
    return jax.shard_map(
        body, mesh=mesh, in_specs=placed, out_specs=P("blk", "mc"), check_vma=False
    )
```

```python
import functools

import jax
import jax.numpy as jnp
from jax import lax
from jax.experimental import pallas as pl
from jax.experimental.pallas import tpu as pltpu
from jax.sharding import PartitionSpec as P

freedom = 4.0
vmem = pl.BlockSpec(memory_space=pltpu.VMEM)
smem = pl.BlockSpec(memory_space=pltpu.SMEM)
anywhere = pl.BlockSpec(memory_space=pl.ANY)
iota = lax.broadcasted_iota


def budget(megabytes):
    return pltpu.CompilerParams(vmem_limit_bytes=megabytes * 1024 * 1024)


def in_hbm(values):
    return pltpu.with_memory_space_constraint(values, pltpu.HBM)


def in_vmem(values):
    return pltpu.with_memory_space_constraint(values, pltpu.VMEM)


def plan_kernel(
    owners, capacity, noise_ref, own_hbm, near_hbm, home_hbm, latent_hbm, outbox_ref, spot_ref, noise_row_ref, latent_ref, own_ref, near_ref, home_ref, sems
):
    per_owner = latent_ref.shape[0]
    copies = [
        pltpu.make_async_copy(home_hbm, home_ref, sems.at[0]),
        pltpu.make_async_copy(own_hbm, own_ref, sems.at[1]),
        pltpu.make_async_copy(near_hbm, near_ref, sems.at[2]),
        pltpu.make_async_copy(latent_hbm, latent_ref, sems.at[3]),
    ]
    for copy in copies:
        copy.start()
    for copy in copies[:3]:
        copy.wait()
    home = home_ref[...]
    high_count, low_count = home.shape
    dest_table = (home // per_owner).astype(jnp.float32).T.astype(jnp.bfloat16)
    slot_table = (home % per_owner).astype(jnp.float32).T.astype(jnp.bfloat16)
    rows = own_ref.shape[1]
    earlier = (iota(jnp.int32, (rows, rows), 0) < iota(jnp.int32, (rows, rows), 1)).astype(jnp.bfloat16)
    high_iota = iota(jnp.int32, (high_count, rows), 0)
    low_iota = iota(jnp.int32, (low_count, rows), 0)
    dest_iota = iota(jnp.int32, (owners, rows), 0)
    before = jnp.zeros((owners, 1), jnp.float32)
    marks = [jnp.zeros((owners, 1), jnp.float32) for _ in range(capacity)]
    for which in range(1 + near_ref.shape[0]):
        ids = own_ref[...] if which == 0 else near_ref[which - 1 : which, :]
        high_hot = (high_iota == ids // low_count).astype(jnp.bfloat16)
        low_hot = low_iota == ids % low_count
        dest = jnp.dot(dest_table, high_hot, preferred_element_type=jnp.float32)
        dest = jnp.sum(jnp.where(low_hot, dest, 0.0), axis=0, keepdims=True)
        slot = jnp.dot(slot_table, high_hot, preferred_element_type=jnp.float32)
        slot = jnp.sum(jnp.where(low_hot, slot, 0.0), axis=0, keepdims=True)
        asked = dest_iota == dest.astype(jnp.int32)
        ranks = before + jnp.dot(asked.astype(jnp.bfloat16), earlier, preferred_element_type=jnp.float32)
        before = before + jnp.sum(asked.astype(jnp.float32), axis=1, keepdims=True)
        for k in range(capacity):
            taken = asked & (ranks == float(k))
            marks[k] = marks[k] + jnp.sum(jnp.where(taken, slot + 1.0, 0.0), axis=1, keepdims=True)
        rank = jnp.sum(jnp.where(asked, ranks, 0.0), axis=0, keepdims=True)
        spot_ref[which : which + 1, :] = (dest * 8.0 + rank).astype(jnp.int32)
    lanes = iota(jnp.int32, (owners, outbox_ref.shape[2]), 1)
    outbox = jnp.full(lanes.shape, -1.0, jnp.float32)
    for k in range(capacity):
        outbox = jnp.where(lanes == k, marks[k] - 1.0, outbox)
    outbox_ref[:, 0, :] = outbox.astype(jnp.int32)
    noise_row_ref[...] = jnp.full(noise_row_ref.shape, noise_ref[0], jnp.float32)
    copies[3].wait()


def pack_kernel(slots_ref, latent_ref, out_ref, turned_ref, scalar_ref, sem):
    owners, capacity = out_ref.shape[:2]
    turned = jnp.maximum(slots_ref[:, 0, :], 0).astype(jnp.float32).T
    turned_ref[:, pl.ds(0, owners)] = turned[: turned_ref.shape[0]].astype(jnp.int32)
    copy = pltpu.make_async_copy(turned_ref, scalar_ref, sem)
    copy.start()
    copy.wait()

    def step(dev, carry):
        for k in range(capacity):
            out_ref[dev, k] = latent_ref[scalar_ref[k, dev]]
        return carry

    lax.fori_loop(0, owners, step, 0, unroll=8)


def score_kernel(
    chunk, spot_ref, noise_ref, obs_ref, fetched_ref, diag_ref, cond_ref, sums_ref
):
    noise = noise_ref[...]
    draw_count = float(fetched_ref.shape[2])
    row_count, width = diag_ref.shape[:2]
    lower = iota(jnp.int32, (width, width), 0) >= iota(jnp.int32, (width, width), 1)
    turned = (((1,), (1,)), ((), ()))
    cut = width // 2

    def score(row):
        spots = [spot_ref[which, row] for which in range(1 + cond_ref.shape[1])]
        panels = [fetched_ref[spot // 8, spot % 8] for spot in spots]
        factor = jnp.where(lower, diag_ref[row], jnp.zeros((), diag_ref.dtype))
        whitened = lax.dot_general(factor, panels[0], turned, preferred_element_type=jnp.float32).T
        top = lax.dot_general(cond_ref[row, 0, pl.ds(0, cut)], panels[1], turned, preferred_element_type=jnp.float32).T
        low = lax.dot_general(panels[1], cond_ref[row, 0, pl.ds(cut, cut)], turned, preferred_element_type=jnp.float32)
        whitened = whitened + jnp.concatenate([top, low], axis=1)
        for which in range(1, cond_ref.shape[1]):
            whitened = whitened + lax.dot_general(
                panels[which + 1], cond_ref[row, which], turned, preferred_element_type=jnp.float32
            )
        scored = (freedom + 1.0) * whitened / (freedom + whitened * whitened)
        scored = scored.astype(jnp.bfloat16).astype(jnp.float32)
        sums_ref[0, pl.ds(row, 1), :] = jnp.sum(scored, axis=0, keepdims=True)
        owned = jnp.sum(panels[0].astype(jnp.float32), axis=0, keepdims=True)
        sums_ref[1, pl.ds(row, 1), :] = noise * (obs_ref[pl.ds(row, 1), :] * draw_count - owned)

    def step(index, carry):
        for i in range(chunk):
            score(index * chunk + i)
        return carry

    lax.fori_loop(0, row_count // chunk, step, 0)


def term_kernel(draws, chunk, spot_ref, mine_ref, other_ref, diag_ref, cond_ref, out_ref, likely_ref):
    row_count, width = diag_ref.shape[:2]
    half = likely_ref.shape[1]
    first = pl.multiple_of(lax.axis_index("mc") * half, half)
    columns = pl.ds(first, half)
    lower = iota(jnp.int32, (width, half), 0) >= iota(jnp.int32, (width, half), 1) + first
    inverse_draws = 1.0 / draws
    which_row = iota(jnp.int32, (16, width), 0)
    out_ref[...] = jnp.zeros_like(out_ref)
    likely_ref[...] = mine_ref[1, :, columns] + other_ref[1, :, columns]

    def term(row):
        total = mine_ref[0, pl.ds(row, 1), :] + other_ref[0, pl.ds(row, 1), :]
        coarse = total.astype(jnp.bfloat16).astype(jnp.float32)
        pieces = jnp.where(which_row == 0, coarse, jnp.where(which_row == 1, total - coarse, 0.0))
        pieces = pieces.astype(jnp.bfloat16)
        for which in range(1 + cond_ref.shape[1]):
            if which == 0:
                factor = jnp.where(lower, diag_ref[row, :, columns], jnp.zeros((), diag_ref.dtype))
            else:
                factor = cond_ref[row, which - 1, :, columns]
            back = jnp.dot(pieces, factor, preferred_element_type=jnp.float32)
            back = back[0:1] + back[1:2]
            if which == 0:
                back = back - likely_ref[pl.ds(row, 1), :]
            spot = spot_ref[which, row]
            place = pl.multiple_of((spot % 8) * half, half)
            out_ref[spot // 8, :, pl.ds(place, half)] = back * -inverse_draws

    def step(index, carry):
        for i in range(chunk):
            term(index * chunk + i)
        return carry

    lax.fori_loop(0, row_count // chunk, step, 0)


def gather_kernel(slots_ref, inbox_ref, out_ref):
    owners = inbox_ref.shape[0]
    per_owner, half = out_ref.shape
    capacity = inbox_ref.shape[2] // half
    slots = slots_ref[:, 0, :].astype(jnp.float32).T
    slots = jnp.concatenate([slots[k : k + 1, :] for k in range(capacity)], axis=1)
    places = iota(jnp.int32, (per_owner, owners * capacity), 0).astype(jnp.float32)
    hot = (places == slots).astype(jnp.bfloat16)
    rest = jnp.concatenate([inbox_ref[:, 0, pl.ds(k * half, half)] for k in range(capacity)], axis=0)
    total = jnp.zeros((per_owner, half), jnp.float32)
    for _ in range(3):
        piece = rest.astype(jnp.bfloat16)
        rest = rest - piece.astype(jnp.float32)
        total = total + jnp.dot(hot, piece, preferred_element_type=jnp.float32)
    out_ref[...] = total


def body(batch_ids, cond_ids, home, latent, diag_factor, cond_factor, obs, noise_prec):
    owners = lax.axis_size("blk")
    groups = lax.axis_size("mc")
    per_owner, draw_count, width = latent.shape
    row_count = batch_ids.shape[0]
    want_kinds = 1 + cond_ids.shape[1]
    capacity = max(2, 10 * row_count // owners)
    draws = draw_count * groups
    half = width // groups

    def swap(values):
        return lax.all_to_all(values, "blk", split_axis=0, concat_axis=0, tiled=True)

    outbox, spot, noise_row, staged = pl.pallas_call(
        functools.partial(plan_kernel, owners, capacity),
        out_shape=(
            jax.ShapeDtypeStruct((owners, 1, 128), jnp.int32),
            jax.ShapeDtypeStruct((want_kinds, row_count), jnp.int32),
            jax.ShapeDtypeStruct((1, width), jnp.float32),
            pltpu.VMEM(latent.shape, latent.dtype),
        ),
        in_specs=[smem] + [anywhere] * 4,
        out_specs=(vmem,) * 4,
        scratch_shapes=[
            pltpu.VMEM((1, row_count), jnp.int32),
            pltpu.VMEM((want_kinds - 1, row_count), jnp.int32),
            pltpu.VMEM((home.shape[0] // 128, 128), jnp.int32),
            pltpu.SemaphoreType.DMA((4,)),
        ],
        compiler_params=budget(16),
        name="plan",
    )(noise_prec.reshape(1), in_hbm(batch_ids.reshape(1, row_count)), in_hbm(cond_ids.T), in_hbm(home.reshape(-1, 128)), in_hbm(latent))
    slots = swap(outbox)
    outgoing = pl.pallas_call(
        pack_kernel,
        out_shape=jax.ShapeDtypeStruct((owners, capacity, draw_count, width), latent.dtype),
        in_specs=[vmem, vmem],
        out_specs=vmem,
        scratch_shapes=[
            pltpu.VMEM((8, 128), jnp.int32),
            pltpu.SMEM((8, 128), jnp.int32),
            pltpu.SemaphoreType.DMA,
        ],
        compiler_params=budget(8),
        cost_estimate=pl.CostEstimate(flops=10**11, transcendentals=0, bytes_accessed=10**8),
        name="pack",
    )(slots, staged)
    fetched = swap(outgoing)
    diag_here, cond_here, obs = in_vmem(diag_factor), in_vmem(cond_factor), in_hbm(obs)
    sums = pl.pallas_call(
        functools.partial(score_kernel, 32),
        out_shape=jax.ShapeDtypeStruct((2, row_count, width), jnp.float32),
        in_specs=[smem] + [vmem] * 5,
        out_specs=vmem,
        compiler_params=budget(12),
        name="score",
    )(spot, noise_row, obs, fetched, diag_here, cond_here)
    others = lax.ppermute(sums, "mc", [(0, 1), (1, 0)])
    terms = pl.pallas_call(
        functools.partial(term_kernel, draws, 32),
        out_shape=jax.ShapeDtypeStruct((owners, 1, capacity * half), jnp.float32),
        in_specs=[smem] + [vmem] * 4,
        out_specs=vmem,
        scratch_shapes=[pltpu.VMEM((row_count, half), jnp.float32)],
        compiler_params=budget(12),
        name="terms",
    )(spot, sums, others, diag_here, cond_here)
    inbox = swap(terms)
    return pl.pallas_call(
        gather_kernel,
        out_shape=jax.ShapeDtypeStruct((per_owner, half), jnp.float32),
        in_specs=[vmem] * 2,
        out_specs=vmem,
        compiler_params=budget(16),
        name="collect",
    )(slots, inbox)


def solution(mesh):
    placed = (
        P("blk"),
        P("blk", None),
        P(),
        P("blk", "mc", None),
        P("blk", None, None),
        P("blk", None, None, None),
        P("blk", None),
        P(),
    )
    return jax.shard_map(
        body, mesh=mesh, in_specs=placed, out_specs=P("blk", "mc"), check_vma=False
    )
```

```python
import functools

import jax
import jax.numpy as jnp
from jax import lax
from jax.experimental import pallas as pl
from jax.experimental.pallas import tpu as pltpu
from jax.sharding import PartitionSpec as P

freedom = 4.0
vmem = pl.BlockSpec(memory_space=pltpu.VMEM)
smem = pl.BlockSpec(memory_space=pltpu.SMEM)
anywhere = pl.BlockSpec(memory_space=pl.ANY)
iota = lax.broadcasted_iota


def budget(megabytes):
    return pltpu.CompilerParams(vmem_limit_bytes=megabytes * 1024 * 1024)


def in_hbm(values):
    return pltpu.with_memory_space_constraint(values, pltpu.HBM)


def in_vmem(values):
    return pltpu.with_memory_space_constraint(values, pltpu.VMEM)


def plan_kernel(
    owners, capacity, noise_ref, own_hbm, near_hbm, home_hbm, latent_hbm, outbox_ref, spot_ref, noise_row_ref, latent_ref, own_ref, near_ref, home_ref, sems
):
    per_owner = latent_ref.shape[0]
    copies = [
        pltpu.make_async_copy(home_hbm, home_ref, sems.at[0]),
        pltpu.make_async_copy(own_hbm, own_ref, sems.at[1]),
        pltpu.make_async_copy(near_hbm, near_ref, sems.at[2]),
        pltpu.make_async_copy(latent_hbm, latent_ref, sems.at[3]),
    ]
    for copy in copies:
        copy.start()
    for copy in copies[:3]:
        copy.wait()
    home = home_ref[...]
    high_count, low_count = home.shape
    dest_table = (home // per_owner).astype(jnp.float32).T.astype(jnp.bfloat16)
    slot_table = (home % per_owner).astype(jnp.float32).T.astype(jnp.bfloat16)
    rows = own_ref.shape[1]
    earlier = (iota(jnp.int32, (rows, rows), 0) < iota(jnp.int32, (rows, rows), 1)).astype(jnp.bfloat16)
    high_iota = iota(jnp.int32, (high_count, rows), 0)
    low_iota = iota(jnp.int32, (low_count, rows), 0)
    dest_iota = iota(jnp.int32, (owners, rows), 0)
    before = jnp.zeros((owners, 1), jnp.float32)
    marks = [jnp.zeros((owners, 1), jnp.float32) for _ in range(capacity)]
    for which in range(1 + near_ref.shape[0]):
        ids = own_ref[...] if which == 0 else near_ref[which - 1 : which, :]
        high_hot = (high_iota == ids // low_count).astype(jnp.bfloat16)
        low_hot = low_iota == ids % low_count
        dest = jnp.dot(dest_table, high_hot, preferred_element_type=jnp.float32)
        dest = jnp.sum(jnp.where(low_hot, dest, 0.0), axis=0, keepdims=True)
        slot = jnp.dot(slot_table, high_hot, preferred_element_type=jnp.float32)
        slot = jnp.sum(jnp.where(low_hot, slot, 0.0), axis=0, keepdims=True)
        asked = dest_iota == dest.astype(jnp.int32)
        ranks = before + jnp.dot(asked.astype(jnp.bfloat16), earlier, preferred_element_type=jnp.float32)
        before = before + jnp.sum(asked.astype(jnp.float32), axis=1, keepdims=True)
        for k in range(capacity):
            taken = asked & (ranks == float(k))
            marks[k] = marks[k] + jnp.sum(jnp.where(taken, slot + 1.0, 0.0), axis=1, keepdims=True)
        rank = jnp.sum(jnp.where(asked, ranks, 0.0), axis=0, keepdims=True)
        spot_ref[which : which + 1, :] = (dest * 8.0 + rank).astype(jnp.int32)
    lanes = iota(jnp.int32, (owners, outbox_ref.shape[2]), 1)
    outbox = jnp.full(lanes.shape, -1.0, jnp.float32)
    for k in range(capacity):
        outbox = jnp.where(lanes == k, marks[k] - 1.0, outbox)
    outbox_ref[:, 0, :] = outbox.astype(jnp.int32)
    noise_row_ref[...] = jnp.full(noise_row_ref.shape, noise_ref[0], jnp.float32)
    copies[3].wait()


def pack_kernel(slots_ref, latent_ref, out_ref, turned_ref, scalar_ref, sem):
    owners, capacity = out_ref.shape[:2]
    turned = jnp.maximum(slots_ref[:, 0, :], 0).astype(jnp.float32).T
    turned_ref[:, pl.ds(0, owners)] = turned[: turned_ref.shape[0]].astype(jnp.int32)
    copy = pltpu.make_async_copy(turned_ref, scalar_ref, sem)
    copy.start()
    copy.wait()

    def step(dev, carry):
        for k in range(capacity):
            out_ref[dev, k] = latent_ref[scalar_ref[k, dev]]
        return carry

    lax.fori_loop(0, owners, step, 0, unroll=8)


def score_kernel(
    chunk, spot_ref, noise_ref, obs_ref, fetched_ref, diag_ref, cond_ref, sums_ref
):
    noise = noise_ref[...]
    draw_count = float(fetched_ref.shape[2])
    row_count, width = diag_ref.shape[:2]
    lower = iota(jnp.int32, (width, width), 0) >= iota(jnp.int32, (width, width), 1)
    turned = (((1,), (1,)), ((), ()))
    cut = width // 2

    def score(row):
        spots = [spot_ref[which, row] for which in range(1 + cond_ref.shape[1])]
        panels = [fetched_ref[spot // 8, spot % 8] for spot in spots]
        factor = jnp.where(lower, diag_ref[row], jnp.zeros((), diag_ref.dtype))
        whitened = lax.dot_general(factor, panels[0], turned, preferred_element_type=jnp.float32).T
        top = lax.dot_general(cond_ref[row, 0, pl.ds(0, cut)], panels[1], turned, preferred_element_type=jnp.float32).T
        low = lax.dot_general(panels[1], cond_ref[row, 0, pl.ds(cut, cut)], turned, preferred_element_type=jnp.float32)
        whitened = whitened + jnp.concatenate([top, low], axis=1)
        for which in range(1, cond_ref.shape[1]):
            whitened = whitened + lax.dot_general(
                panels[which + 1], cond_ref[row, which], turned, preferred_element_type=jnp.float32
            )
        scored = (freedom + 1.0) * whitened / (freedom + whitened * whitened)
        scored = scored.astype(jnp.bfloat16).astype(jnp.float32)
        sums_ref[0, pl.ds(row, 1), :] = jnp.sum(scored, axis=0, keepdims=True)
        owned = jnp.sum(panels[0].astype(jnp.float32), axis=0, keepdims=True)
        sums_ref[1, pl.ds(row, 1), :] = noise * (obs_ref[pl.ds(row, 1), :] * draw_count - owned)

    def step(index, carry):
        for i in range(chunk):
            score(index * chunk + i)
        return carry

    lax.fori_loop(0, row_count // chunk, step, 0)


def term_kernel(draws, chunk, spot_ref, mine_ref, other_ref, diag_ref, cond_ref, out_ref, likely_ref):
    row_count, width = diag_ref.shape[:2]
    half = likely_ref.shape[1]
    first = pl.multiple_of(lax.axis_index("mc") * half, half)
    columns = pl.ds(first, half)
    lower = iota(jnp.int32, (width, half), 0) >= iota(jnp.int32, (width, half), 1) + first
    inverse_draws = 1.0 / draws
    which_row = iota(jnp.int32, (16, width), 0)
    out_ref[...] = jnp.zeros_like(out_ref)
    likely_ref[...] = mine_ref[1, :, columns] + other_ref[1, :, columns]

    def term(row):
        total = mine_ref[0, pl.ds(row, 1), :] + other_ref[0, pl.ds(row, 1), :]
        coarse = total.astype(jnp.bfloat16).astype(jnp.float32)
        pieces = jnp.where(which_row == 0, coarse, jnp.where(which_row == 1, total - coarse, 0.0))
        pieces = pieces.astype(jnp.bfloat16)
        for which in range(1 + cond_ref.shape[1]):
            if which == 0:
                factor = jnp.where(lower, diag_ref[row, :, columns], jnp.zeros((), diag_ref.dtype))
            else:
                factor = cond_ref[row, which - 1, :, columns]
            back = jnp.dot(pieces, factor, preferred_element_type=jnp.float32)
            back = back[0:1] + back[1:2]
            if which == 0:
                back = back - likely_ref[pl.ds(row, 1), :]
            spot = spot_ref[which, row]
            place = pl.multiple_of((spot % 8) * half, half)
            out_ref[spot // 8, :, pl.ds(place, half)] = back * -inverse_draws

    def step(index, carry):
        for i in range(chunk):
            term(index * chunk + i)
        return carry

    lax.fori_loop(0, row_count // chunk, step, 0)


def gather_kernel(slots_ref, inbox_ref, out_ref):
    owners = inbox_ref.shape[0]
    per_owner, half = out_ref.shape
    capacity = inbox_ref.shape[2] // half
    slots = slots_ref[:, 0, :].astype(jnp.float32).T
    slots = jnp.concatenate([slots[k : k + 1, :] for k in range(capacity)], axis=1)
    places = iota(jnp.int32, (per_owner, owners * capacity), 0).astype(jnp.float32)
    hot = (places == slots).astype(jnp.bfloat16)
    rest = jnp.concatenate([inbox_ref[:, 0, pl.ds(k * half, half)] for k in range(capacity)], axis=0)
    total = jnp.zeros((per_owner, half), jnp.float32)
    for _ in range(3):
        piece = rest.astype(jnp.bfloat16)
        rest = rest - piece.astype(jnp.float32)
        total = total + jnp.dot(hot, piece, preferred_element_type=jnp.float32)
    out_ref[...] = total


def body(batch_ids, cond_ids, home, latent, diag_factor, cond_factor, obs, noise_prec):
    owners = lax.axis_size("blk")
    groups = lax.axis_size("mc")
    per_owner, draw_count, width = latent.shape
    row_count = batch_ids.shape[0]
    want_kinds = 1 + cond_ids.shape[1]
    capacity = max(2, 10 * row_count // owners)
    draws = draw_count * groups
    half = width // groups

    def swap(values):
        return lax.all_to_all(values, "blk", split_axis=0, concat_axis=0, tiled=True)

    outbox, spot, noise_row, staged = pl.pallas_call(
        functools.partial(plan_kernel, owners, capacity),
        out_shape=(
            jax.ShapeDtypeStruct((owners, 1, 8), jnp.int32),
            jax.ShapeDtypeStruct((want_kinds, row_count), jnp.int32),
            jax.ShapeDtypeStruct((1, width), jnp.float32),
            pltpu.VMEM(latent.shape, latent.dtype),
        ),
        in_specs=[smem] + [anywhere] * 4,
        out_specs=(vmem,) * 4,
        scratch_shapes=[
            pltpu.VMEM((1, row_count), jnp.int32),
            pltpu.VMEM((want_kinds - 1, row_count), jnp.int32),
            pltpu.VMEM((home.shape[0] // 128, 128), jnp.int32),
            pltpu.SemaphoreType.DMA((4,)),
        ],
        compiler_params=budget(16),
        name="plan",
    )(noise_prec.reshape(1), in_hbm(batch_ids.reshape(1, row_count)), in_hbm(cond_ids.T), in_hbm(home.reshape(-1, 128)), in_hbm(latent))
    slots = swap(outbox)
    outgoing = pl.pallas_call(
        pack_kernel,
        out_shape=jax.ShapeDtypeStruct((owners, capacity, draw_count, width), latent.dtype),
        in_specs=[vmem, vmem],
        out_specs=vmem,
        scratch_shapes=[
            pltpu.VMEM((8, 128), jnp.int32),
            pltpu.SMEM((8, 128), jnp.int32),
            pltpu.SemaphoreType.DMA,
        ],
        compiler_params=budget(8),
        cost_estimate=pl.CostEstimate(flops=10**11, transcendentals=0, bytes_accessed=10**8),
        name="pack",
    )(slots, staged)
    fetched = swap(outgoing)
    diag_here, cond_here, obs = in_vmem(diag_factor), in_vmem(cond_factor), in_hbm(obs)
    sums = pl.pallas_call(
        functools.partial(score_kernel, 32),
        out_shape=jax.ShapeDtypeStruct((2, row_count, width), jnp.float32),
        in_specs=[smem] + [vmem] * 5,
        out_specs=vmem,
        compiler_params=budget(12),
        name="score",
    )(spot, noise_row, obs, fetched, diag_here, cond_here)
    others = lax.ppermute(sums, "mc", [(0, 1), (1, 0)])
    terms = pl.pallas_call(
        functools.partial(term_kernel, draws, 32),
        out_shape=jax.ShapeDtypeStruct((owners, 1, capacity * half), jnp.float32),
        in_specs=[smem] + [vmem] * 4,
        out_specs=vmem,
        scratch_shapes=[pltpu.VMEM((row_count, half), jnp.float32)],
        compiler_params=budget(12),
        name="terms",
    )(spot, sums, others, diag_here, cond_here)
    inbox = swap(terms)
    return pl.pallas_call(
        gather_kernel,
        out_shape=jax.ShapeDtypeStruct((per_owner, half), jnp.float32),
        in_specs=[vmem] * 2,
        out_specs=vmem,
        compiler_params=budget(16),
        name="collect",
    )(slots, inbox)


def solution(mesh):
    placed = (
        P("blk"),
        P("blk", None),
        P(),
        P("blk", "mc", None),
        P("blk", None, None),
        P("blk", None, None, None),
        P("blk", None),
        P(),
    )
    return jax.shard_map(
        body, mesh=mesh, in_specs=placed, out_specs=P("blk", "mc"), check_vma=False
    )
```

```python
import functools

import jax
import jax.numpy as jnp
from jax import lax
from jax.experimental import pallas as pl
from jax.experimental.pallas import tpu as pltpu
from jax.sharding import PartitionSpec as P

freedom = 4.0
vmem = pl.BlockSpec(memory_space=pltpu.VMEM)
smem = pl.BlockSpec(memory_space=pltpu.SMEM)
anywhere = pl.BlockSpec(memory_space=pl.ANY)
iota = lax.broadcasted_iota


def budget(megabytes):
    return pltpu.CompilerParams(vmem_limit_bytes=megabytes * 1024 * 1024)


def in_hbm(values):
    return pltpu.with_memory_space_constraint(values, pltpu.HBM)


def in_vmem(values):
    return pltpu.with_memory_space_constraint(values, pltpu.VMEM)


def plan_kernel(
    owners, capacity, noise_ref, own_hbm, near_hbm, home_hbm, latent_hbm, outbox_ref, spot_ref, noise_row_ref, latent_ref, own_ref, near_ref, home_ref, sems
):
    per_owner = latent_ref.shape[0]
    copies = [
        pltpu.make_async_copy(home_hbm, home_ref, sems.at[0]),
        pltpu.make_async_copy(own_hbm, own_ref, sems.at[1]),
        pltpu.make_async_copy(near_hbm, near_ref, sems.at[2]),
        pltpu.make_async_copy(latent_hbm, latent_ref, sems.at[3]),
    ]
    for copy in copies:
        copy.start()
    for copy in copies[:3]:
        copy.wait()
    home = home_ref[...]
    high_count, low_count = home.shape
    dest_table = (home // per_owner).astype(jnp.float32).T.astype(jnp.bfloat16)
    slot_table = (home % per_owner).astype(jnp.float32).T.astype(jnp.bfloat16)
    rows = own_ref.shape[1]
    earlier = (iota(jnp.int32, (rows, rows), 0) < iota(jnp.int32, (rows, rows), 1)).astype(jnp.bfloat16)
    high_iota = iota(jnp.int32, (high_count, rows), 0)
    low_iota = iota(jnp.int32, (low_count, rows), 0)
    dest_iota = iota(jnp.int32, (owners, rows), 0)
    before = jnp.zeros((owners, 1), jnp.float32)
    marks = [jnp.zeros((owners, 1), jnp.float32) for _ in range(capacity)]
    for which in range(1 + near_ref.shape[0]):
        ids = own_ref[...] if which == 0 else near_ref[which - 1 : which, :]
        high_hot = (high_iota == ids // low_count).astype(jnp.bfloat16)
        low_hot = low_iota == ids % low_count
        dest = jnp.dot(dest_table, high_hot, preferred_element_type=jnp.float32)
        dest = jnp.sum(jnp.where(low_hot, dest, 0.0), axis=0, keepdims=True)
        slot = jnp.dot(slot_table, high_hot, preferred_element_type=jnp.float32)
        slot = jnp.sum(jnp.where(low_hot, slot, 0.0), axis=0, keepdims=True)
        asked = dest_iota == dest.astype(jnp.int32)
        ranks = before + jnp.dot(asked.astype(jnp.bfloat16), earlier, preferred_element_type=jnp.float32)
        before = before + jnp.sum(asked.astype(jnp.float32), axis=1, keepdims=True)
        for k in range(capacity):
            taken = asked & (ranks == float(k))
            marks[k] = marks[k] + jnp.sum(jnp.where(taken, slot + 1.0, 0.0), axis=1, keepdims=True)
        rank = jnp.sum(jnp.where(asked, ranks, 0.0), axis=0, keepdims=True)
        spot_ref[which : which + 1, :] = (dest * 8.0 + rank).astype(jnp.int32)
    lanes = iota(jnp.int32, (owners, outbox_ref.shape[2]), 1)
    outbox = jnp.full(lanes.shape, -1.0, jnp.float32)
    for k in range(capacity):
        outbox = jnp.where(lanes == k, marks[k] - 1.0, outbox)
    outbox_ref[:, 0, :] = outbox.astype(jnp.int32)
    noise_row_ref[...] = jnp.full(noise_row_ref.shape, noise_ref[0], jnp.float32)
    copies[3].wait()


def pack_kernel(slots_ref, latent_ref, out_ref, turned_ref, scalar_ref, sem):
    owners, capacity = out_ref.shape[:2]
    turned = jnp.maximum(slots_ref[:, 0, :], 0).astype(jnp.float32).T
    turned_ref[:, pl.ds(0, owners)] = turned[: turned_ref.shape[0]].astype(jnp.int32)
    copy = pltpu.make_async_copy(turned_ref, scalar_ref, sem)
    copy.start()
    copy.wait()

    def step(dev, carry):
        for k in range(capacity):
            out_ref[dev, k] = latent_ref[scalar_ref[k, dev]]
        return carry

    lax.fori_loop(0, owners, step, 0, unroll=8)


def score_kernel(
    chunk, spot_ref, noise_ref, obs_ref, fetched_ref, diag_ref, cond_ref, sums_ref
):
    noise = noise_ref[...]
    draw_count = float(fetched_ref.shape[2])
    row_count, width = diag_ref.shape[:2]
    lower = iota(jnp.int32, (width, width), 0) >= iota(jnp.int32, (width, width), 1)
    turned = (((1,), (1,)), ((), ()))
    cut = width // 2

    def score(row):
        spots = [spot_ref[which, row] for which in range(1 + cond_ref.shape[1])]
        panels = [fetched_ref[spot // 8, spot % 8] for spot in spots]
        factor = jnp.where(lower, diag_ref[row], jnp.zeros((), diag_ref.dtype))
        whitened = lax.dot_general(factor, panels[0], turned, preferred_element_type=jnp.float32).T
        top = lax.dot_general(cond_ref[row, 0, pl.ds(0, cut)], panels[1], turned, preferred_element_type=jnp.float32).T
        low = lax.dot_general(panels[1], cond_ref[row, 0, pl.ds(cut, cut)], turned, preferred_element_type=jnp.float32)
        whitened = whitened + jnp.concatenate([top, low], axis=1)
        for which in range(1, cond_ref.shape[1]):
            whitened = whitened + lax.dot_general(
                panels[which + 1], cond_ref[row, which], turned, preferred_element_type=jnp.float32
            )
        scored = (freedom + 1.0) * whitened / (freedom + whitened * whitened)
        scored = scored.astype(jnp.bfloat16).astype(jnp.float32)
        sums_ref[0, pl.ds(row, 1), :] = jnp.sum(scored, axis=0, keepdims=True)
        owned = jnp.sum(panels[0].astype(jnp.float32), axis=0, keepdims=True)
        sums_ref[1, pl.ds(row, 1), :] = noise * (obs_ref[pl.ds(row, 1), :] * draw_count - owned)

    def step(index, carry):
        for i in range(chunk):
            score(index * chunk + i)
        return carry

    lax.fori_loop(0, row_count // chunk, step, 0)


def term_kernel(draws, chunk, spot_ref, mine_ref, other_ref, diag_ref, cond_ref, out_ref, likely_ref):
    row_count, width = diag_ref.shape[:2]
    half = likely_ref.shape[1]
    first = pl.multiple_of(lax.axis_index("mc") * half, half)
    columns = pl.ds(first, half)
    lower = iota(jnp.int32, (width, half), 0) >= iota(jnp.int32, (width, half), 1) + first
    inverse_draws = 1.0 / draws
    which_row = iota(jnp.int32, (16, width), 0)
    out_ref[...] = jnp.zeros_like(out_ref)
    likely_ref[...] = mine_ref[1, :, columns] + other_ref[1, :, columns]

    def term(row):
        total = mine_ref[0, pl.ds(row, 1), :] + other_ref[0, pl.ds(row, 1), :]
        coarse = total.astype(jnp.bfloat16).astype(jnp.float32)
        pieces = jnp.where(which_row == 0, coarse, jnp.where(which_row == 1, total - coarse, 0.0))
        pieces = pieces.astype(jnp.bfloat16)
        for which in range(1 + cond_ref.shape[1]):
            if which == 0:
                factor = jnp.where(lower, diag_ref[row, :, columns], jnp.zeros((), diag_ref.dtype))
            else:
                factor = cond_ref[row, which - 1, :, columns]
            back = jnp.dot(pieces, factor, preferred_element_type=jnp.float32)
            back = back[0:1] + back[1:2]
            if which == 0:
                back = back - likely_ref[pl.ds(row, 1), :]
            spot = spot_ref[which, row]
            place = pl.multiple_of((spot % 8) * half, half)
            out_ref[spot // 8, :, pl.ds(place, half)] = back * -inverse_draws

    def step(index, carry):
        for i in range(chunk):
            term(index * chunk + i)
        return carry

    lax.fori_loop(0, row_count // chunk, step, 0)


def gather_kernel(slots_ref, inbox_ref, out_ref):
    owners = inbox_ref.shape[0]
    per_owner, half = out_ref.shape
    capacity = inbox_ref.shape[2] // half
    slots = slots_ref[:, 0, :].astype(jnp.float32).T
    slots = jnp.concatenate([slots[k : k + 1, :] for k in range(capacity)], axis=1)
    places = iota(jnp.int32, (per_owner, owners * capacity), 0).astype(jnp.float32)
    hot = (places == slots).astype(jnp.bfloat16)
    rest = jnp.concatenate([inbox_ref[:, 0, pl.ds(k * half, half)] for k in range(capacity)], axis=0)
    pieces = []
    for _ in range(3):
        piece = rest.astype(jnp.bfloat16)
        rest = rest - piece.astype(jnp.float32)
        pieces.append(piece)
    total = jnp.dot(hot, jnp.concatenate(pieces, axis=1), preferred_element_type=jnp.float32)
    out_ref[...] = total[:, :half] + total[:, half : 2 * half] + total[:, 2 * half :]


def body(batch_ids, cond_ids, home, latent, diag_factor, cond_factor, obs, noise_prec):
    owners = lax.axis_size("blk")
    groups = lax.axis_size("mc")
    per_owner, draw_count, width = latent.shape
    row_count = batch_ids.shape[0]
    want_kinds = 1 + cond_ids.shape[1]
    capacity = max(2, 10 * row_count // owners)
    draws = draw_count * groups
    half = width // groups

    def swap(values):
        return lax.all_to_all(values, "blk", split_axis=0, concat_axis=0, tiled=True)

    outbox, spot, noise_row, staged = pl.pallas_call(
        functools.partial(plan_kernel, owners, capacity),
        out_shape=(
            jax.ShapeDtypeStruct((owners, 1, 8), jnp.int32),
            jax.ShapeDtypeStruct((want_kinds, row_count), jnp.int32),
            jax.ShapeDtypeStruct((1, width), jnp.float32),
            pltpu.VMEM(latent.shape, latent.dtype),
        ),
        in_specs=[smem] + [anywhere] * 4,
        out_specs=(vmem,) * 4,
        scratch_shapes=[
            pltpu.VMEM((1, row_count), jnp.int32),
            pltpu.VMEM((want_kinds - 1, row_count), jnp.int32),
            pltpu.VMEM((home.shape[0] // 128, 128), jnp.int32),
            pltpu.SemaphoreType.DMA((4,)),
        ],
        compiler_params=budget(16),
        name="plan",
    )(noise_prec.reshape(1), in_hbm(batch_ids.reshape(1, row_count)), in_hbm(cond_ids.T), in_hbm(home.reshape(-1, 128)), in_hbm(latent))
    slots = swap(outbox)
    outgoing = pl.pallas_call(
        pack_kernel,
        out_shape=jax.ShapeDtypeStruct((owners, capacity, draw_count, width), latent.dtype),
        in_specs=[vmem, vmem],
        out_specs=vmem,
        scratch_shapes=[
            pltpu.VMEM((8, 128), jnp.int32),
            pltpu.SMEM((8, 128), jnp.int32),
            pltpu.SemaphoreType.DMA,
        ],
        compiler_params=budget(8),
        cost_estimate=pl.CostEstimate(flops=10**11, transcendentals=0, bytes_accessed=10**8),
        name="pack",
    )(slots, staged)
    fetched = swap(outgoing)
    diag_here, cond_here, obs = in_vmem(diag_factor), in_vmem(cond_factor), in_hbm(obs)
    sums = pl.pallas_call(
        functools.partial(score_kernel, 32),
        out_shape=jax.ShapeDtypeStruct((2, row_count, width), jnp.float32),
        in_specs=[smem] + [vmem] * 5,
        out_specs=vmem,
        compiler_params=budget(12),
        name="score",
    )(spot, noise_row, obs, fetched, diag_here, cond_here)
    others = lax.ppermute(sums, "mc", [(0, 1), (1, 0)])
    terms = pl.pallas_call(
        functools.partial(term_kernel, draws, 32),
        out_shape=jax.ShapeDtypeStruct((owners, 1, capacity * half), jnp.float32),
        in_specs=[smem] + [vmem] * 4,
        out_specs=vmem,
        scratch_shapes=[pltpu.VMEM((row_count, half), jnp.float32)],
        compiler_params=budget(12),
        name="terms",
    )(spot, sums, others, diag_here, cond_here)
    inbox = swap(terms)
    return pl.pallas_call(
        gather_kernel,
        out_shape=jax.ShapeDtypeStruct((per_owner, half), jnp.float32),
        in_specs=[vmem] * 2,
        out_specs=vmem,
        compiler_params=budget(16),
        name="collect",
    )(slots, inbox)


def solution(mesh):
    placed = (
        P("blk"),
        P("blk", None),
        P(),
        P("blk", "mc", None),
        P("blk", None, None),
        P("blk", None, None, None),
        P("blk", None),
        P(),
    )
    return jax.shard_map(
        body, mesh=mesh, in_specs=placed, out_specs=P("blk", "mc"), check_vma=False
    )
```
